32 devices in a mesh: parts: 2 (over y), row: 4 (over z), col: 4 (over x, core).
Axes of the slice: x: 2, y: 2, z: 4, core: 2. Of those that a mesh axis runs over, the one named last changes fastest.
Arguments:
- sigma_anc: float32 [24576, 12288], P(('parts', 'row'), 'col'), parts along dimension 0
- normal_factor: float32 [4, 12288, 512], P('parts', ('col', 'row')), parts along dimension 0, may hold values from -0.078125 to 0.078125
- jj_inverse: float32 [4, 512, 512], P('parts', None, 'col'), parts along dimension 0, may hold values from -6 to 6
- blocks: int32 [4, 128], P('parts'), parts along dimension 0, may hold values from 0 to 255, as said below
Outputs:
- sigma_rj: float32 [4, 12288, 512], P('parts', 'row', 'col'), parts along dimension 0
- sigma_jj: float32 [4, 512, 512], P('parts', None, 'col'), parts along dimension 0
The draws below stay inside these ranges and needn't reach their ends.
There are 2 independent parts, one for each index of `parts`. The reference program is written for one: setup_inputs(seed, part) draws one part's arguments, and reference() takes and returns one part's arrays. A program takes and returns all parts, laid end to end along the dimension named above; each array names one. Nothing has to cross between parts.
Inputs may be any that keep to these rules, and one draw needn't show every extreme that they name: Each list names 128 different blocks and always holds block 0 and block 255.
All inputs are finite; a program needn't handle non-finite values.
Results may differ from the reference program's by a relative error of at most 0.0001.
Values sent between devices are 32-bit elements; how exact they have to be, the bound alone decides.
A program may use at most 192 MiB of HBM per device.

```python
import jax
import jax.numpy as jnp
from jax import lax

W = 512
BLK = 48
NBLK = 256
LIST = 128
ANC = 12288


def draw_sigma_anc(key, part):
    raw = jax.random.normal(key, (NBLK * BLK, NBLK * BLK), jnp.float32)
    symmetric = (raw + raw.T) * 0.7071
    rows_iota = lax.broadcasted_iota(jnp.int32, (NBLK * BLK, NBLK * BLK), 0)
    cols_iota = lax.broadcasted_iota(jnp.int32, (NBLK * BLK, NBLK * BLK), 1)
    return symmetric + jnp.where(rows_iota == cols_iota, 8.0, 0.0).astype(jnp.float32)


def draw_blocks(key, part):
    lists = []
    for supernode in range(2):
        shuffled = jax.random.permutation(jax.random.fold_in(key, 17 + supernode), NBLK - 2).astype(jnp.int32)
        inner = shuffled[:LIST - 2] + 1
        ends = jnp.array([0, NBLK - 1], dtype=jnp.int32)
        lists.append(jnp.concatenate([ends, inner]))
    return jnp.stack(lists).astype(jnp.int32)


def steps_of(own_key, extent, cuts, least, high):
    factor_of = 1.0
    for axis_at, parts in cuts:
        heights = jax.random.uniform(jax.random.fold_in(jax.random.fold_in(own_key, 6), axis_at), (parts,), jnp.float32, least / len(cuts), high / len(cuts))
        factor_of = factor_of * jnp.repeat(jnp.exp(heights), extent[axis_at] // parts).reshape((-1,) + (1,) * (len(extent) - 1 - axis_at))
    return factor_of


def gaussian(own_key, extent, width, bound, pieces=(), kind=jnp.bfloat16):
    values = width * jax.random.normal(own_key, extent, jnp.float32)
    if pieces:
        values = values * steps_of(own_key, extent, pieces, -0.22, 0.18)
    return jnp.clip(values, -bound, bound).astype(kind)


def setup_inputs(seed: int = 0, part: int = 0) -> dict:
    splits = jax.random.split(jax.random.key(seed), 5)
    own_keys = jax.random.split(jax.random.fold_in(splits[4], part), 5)
    sigma_anc = draw_sigma_anc(jax.random.fold_in(jax.random.fold_in(splits[4], part), 71), part)
    normal_factor = gaussian(own_keys[1], (2, ANC, W), (LIST * BLK) ** -0.5, 0.078125, ((1, 16),), jnp.float32)
    jj_inverse = gaussian(own_keys[2], (2, W, W), 1.0, 6.0, ((2, 4),), jnp.float32)
    blocks = draw_blocks(jax.random.fold_in(jax.random.fold_in(splits[4], part), 71), part)
    return dict(sigma_anc=sigma_anc, normal_factor=normal_factor, jj_inverse=jj_inverse, blocks=blocks)


def reference(sigma_anc, normal_factor, jj_inverse, blocks):
    block_ids = jnp.arange(NBLK, dtype=jnp.int32)
    rj_list = []
    jj_list = []
    for supernode in range(2):
        listed = jnp.any(blocks[supernode][:, None] == block_ids[None, :], axis=0)
        row_mask = jnp.repeat(listed.astype(jnp.float32), BLK, total_repeat_length=NBLK * BLK)
        masked = normal_factor[supernode] * row_mask[:, None]
        product = jnp.dot(sigma_anc, masked, precision=lax.Precision.HIGHEST, preferred_element_type=jnp.float32)
        sigma_rj = -(product * row_mask[:, None])
        update = jnp.dot(masked.T, sigma_rj, precision=lax.Precision.HIGHEST, preferred_element_type=jnp.float32)
        rj_list.append(sigma_rj)
        jj_list.append(jj_inverse[supernode] - update)
    return jnp.stack(rj_list), jnp.stack(jj_list)
```

```python
import jax
import jax.numpy as jnp
from jax import lax
from jax.sharding import PartitionSpec as P

BLK = 48


def listed_mask(blocks, first_block, count, rows):
    block_ids = first_block + jnp.arange(count, dtype=jnp.int32)
    listed = jnp.any(blocks[:, :, None] == block_ids[None, None, :], axis=1).astype(jnp.float32)
    return jnp.repeat(listed, BLK, axis=1, total_repeat_length=rows)[:, :, None]


def shards(sigma_anc, normal_factor, jj_inverse, blocks):
    tile_rows, tile_cols = sigma_anc.shape
    row_count = lax.axis_size("row")
    row_index = lax.axis_index("row")
    col_index = lax.axis_index("col")
    local_rows = normal_factor.shape[1]
    local_blocks = local_rows // BLK
    first_local = (col_index * row_count + row_index) * local_blocks
    masked = normal_factor * listed_mask(blocks, first_local, local_blocks, local_rows)
    row_blocks = tile_rows // BLK
    row_mask = listed_mask(blocks, row_index * row_blocks, row_blocks, tile_rows)
    start_row = row_index * tile_rows
    root_col = start_row // tile_cols
    offset = jnp.clip(start_row - col_index * tile_cols, 0, tile_cols - tile_rows)
    is_root = (col_index == root_col).astype(jnp.float32)
    rj_list = []
    update_list = []
    for supernode in range(2):
        gathered = lax.all_gather(masked[supernode], "row", axis=0, tiled=True)
        partial = jnp.dot(
            sigma_anc,
            gathered,
            precision=lax.Precision.HIGH,
            preferred_element_type=jnp.float32,
        )
        own_rj = -lax.psum_scatter(partial * row_mask[supernode], "col", scatter_dimension=1, tiled=True)
        rj_list.append(own_rj)
        wide_rj = lax.all_gather(own_rj, "col", axis=1, tiled=True)
        slab = lax.dynamic_slice_in_dim(gathered, offset, tile_rows, 0) * is_root
        update = lax.dot_general(
            slab,
            wide_rj,
            (((0,), (0,)), ((), ())),
            precision=lax.Precision.HIGH,
            preferred_element_type=jnp.float32,
        )
        update_list.append(lax.psum(lax.psum_scatter(update, "col", scatter_dimension=1, tiled=True), "row"))
    return (jnp.stack(rj_list), jj_inverse - jnp.stack(update_list))


def solution(mesh):
    placed = (
        P(("parts", "row"), "col"),
        P("parts", ("col", "row"), None),
        P("parts", None, "col"),
        P("parts", None),
    )
    return jax.shard_map(
        shards,
        mesh=mesh,
        in_specs=placed,
        out_specs=(P("parts", "row", "col"), P("parts", None, "col")),
        check_vma=False,
    )
```

```python
import functools

import jax
import jax.numpy as jnp
from jax import lax
from jax.experimental import pallas as pl
from jax.experimental.pallas import tpu as pltpu
from jax.sharding import PartitionSpec as P

BLK = 48
HALVES = 2
MESH = pl.DeviceIdType.MESH


def listed_mask(blocks, first_block, count, rows):
    block_ids = first_block + jnp.arange(count, dtype=jnp.int32)
    listed = jnp.any(blocks[:, :, None] == block_ids[None, None, :], axis=1).astype(jnp.float32)
    return jnp.repeat(listed, BLK, axis=1, total_repeat_length=rows)


def split(value):
    high = lax.reduce_precision(value, 8, 7)
    return high.astype(jnp.bfloat16), (value - high).astype(jnp.bfloat16)


def dot3(left, right, dims):
    (lh, ll), (rh, rl) = left, right

    def dot(a, b):
        return lax.dot_general(a, b, (dims, ((), ())), preferred_element_type=jnp.float32)

    return dot(lh, rh) + dot(lh, rl) + dot(ll, rh)


def diagonal_kernel(n, u_ref, jj_ref, out_ref, held, send1, recv1, send2, recv2):
    row, col = lax.axis_index("row"), lax.axis_index("col")
    me = row * n + col
    count = n * n
    piece = u_ref.shape[1] // n
    width = u_ref.shape[2] // n
    barrier = pltpu.get_barrier_semaphore()
    for step in range(1, count):
        other = lax.rem(me + step, count)
        pl.semaphore_signal(barrier, inc=1, device_id={"row": other // n, "col": lax.rem(other, n)}, device_id_type=MESH)
    pl.semaphore_wait(barrier, count - 1)

    def part_of(to_row, to_col):
        return u_ref.at[:, pl.ds(pl.multiple_of(to_row * piece, piece), piece), pl.ds(pl.multiple_of(to_col * width, width), width)]

    def scatter(step):
        other = lax.rem(me + step, count)
        to_row, to_col = other // n, lax.rem(other, n)
        return pltpu.make_async_remote_copy(
            src_ref=part_of(to_row, to_col),
            dst_ref=held.at[row],
            send_sem=send1.at[step],
            recv_sem=recv1.at[row],
            device_id={"row": to_row, "col": to_col},
            device_id_type=MESH,
        )

    @pl.when(row == col)
    def _():
        for step in range(1, count):
            scatter(step).start()
        held[row] = part_of(row, col)[...]

    for root in range(n):
        @pl.when(jnp.logical_or(row != root, col != root))
        def _():
            pltpu.make_async_remote_copy(
                src_ref=held.at[root],
                dst_ref=held.at[root],
                send_sem=send1.at[0],
                recv_sem=recv1.at[root],
                device_id={"row": lax.rem(row + 1, n)},
                device_id_type=MESH,
            ).wait_recv()

    mine = pl.ds(pl.multiple_of(row * piece, piece), piece)
    total = held[0]
    for root in range(1, n):
        total = total + held[root]
    out_ref[:, mine, :] = jj_ref[:, mine, :] - total

    def share(step):
        return pltpu.make_async_remote_copy(
            src_ref=out_ref.at[:, mine, :],
            dst_ref=out_ref.at[:, mine, :],
            send_sem=send2.at[step],
            recv_sem=recv2.at[step],
            device_id={"row": lax.rem(row + step, n)},
            device_id_type=MESH,
        )

    for step in range(1, n):
        share(step).start()
    for step in range(1, n):
        share(step).wait()

    @pl.when(row == col)
    def _():
        for step in range(1, count):
            scatter(step).wait_send()


def finish_diagonal(update, jj_inverse, n):
    supernodes, w, part_cols = jj_inverse.shape
    return pl.pallas_call(
        functools.partial(diagonal_kernel, n),
        out_shape=jax.ShapeDtypeStruct(jj_inverse.shape, jnp.float32),
        in_specs=[pl.BlockSpec(memory_space=pltpu.VMEM)] * 2,
        out_specs=pl.BlockSpec(memory_space=pltpu.VMEM),
        scratch_shapes=[
            pltpu.VMEM((n, supernodes, w // n, part_cols), jnp.float32),
            pltpu.SemaphoreType.DMA((n * n,)),
            pltpu.SemaphoreType.DMA((n,)),
            pltpu.SemaphoreType.DMA((n,)),
            pltpu.SemaphoreType.DMA((n,)),
        ],
        compiler_params=pltpu.CompilerParams(collective_id=0, has_side_effects=True),
    )(update, jj_inverse)


def shards(sigma_anc, normal_factor, jj_inverse, blocks):
    tile_rows, tile_cols = sigma_anc.shape
    row_count = lax.axis_size("row")
    col_count = lax.axis_size("col")
    row_index = lax.axis_index("row")
    col_index = lax.axis_index("col")
    supernodes, local_rows, w = normal_factor.shape
    part_cols = jj_inverse.shape[2]
    sub = part_cols // HALVES
    chunk = sub * col_count
    local_blocks = local_rows // BLK
    first_local = (col_index * row_count + row_index) * local_blocks
    masked = normal_factor * listed_mask(blocks, first_local, local_blocks, local_rows)[:, :, None]
    chunks = masked.reshape(supernodes, local_rows, col_count, HALVES, sub).transpose(0, 3, 1, 2, 4)
    chunks = chunks.reshape(supernodes, HALVES, local_rows, chunk)
    row_blocks = tile_rows // BLK
    row_mask = listed_mask(blocks, row_index * row_blocks, row_blocks, tile_rows)
    start_row = row_index * tile_rows
    root_col = start_row // tile_cols
    square = tile_rows == tile_cols
    offset = jnp.clip(start_row - col_index * tile_cols, 0, tile_cols - tile_rows)
    ah, al = split(sigma_anc)
    a3 = jnp.concatenate([ah, ah, al], axis=1)

    def slab_of(value):
        return value if square else lax.dynamic_slice_in_dim(value, offset, tile_rows, 0)

    rj_list = []
    update_list = []
    for supernode in range(supernodes):
        own_list = []
        wide_list = []
        gathered_list = []
        for half in range(HALVES):
            gathered = lax.all_gather(chunks[supernode, half], "row", axis=0, tiled=True)
            bh, bl = split(gathered)
            gathered_list.append((slab_of(bh), slab_of(bl)))
            b3 = jnp.concatenate([bh, bl, bh], axis=0)
            partial = lax.dot_general(b3, a3, (((0,), (1,)), ((), ())), preferred_element_type=jnp.float32)
            own = -lax.psum_scatter(partial * row_mask[supernode][None, :], "col", scatter_dimension=0, tiled=True)
            own_list.append(own)
            wide_list.append(split(lax.all_gather(own, "col", axis=0, tiled=True)))
        rj_list.append(jnp.concatenate(own_list, axis=0).T)
        slab = tuple(jnp.concatenate([g[i] for g in gathered_list], axis=1) for i in range(2))
        update = jnp.stack([dot3(slab, wide, ((0,), (1,))) for wide in wide_list], axis=1)
        update = update.reshape(HALVES, col_count, sub, HALVES, col_count, sub).transpose(1, 0, 2, 4, 3, 5)
        update_list.append(update.reshape(w, w))
    update = jnp.stack(update_list)
    if square and row_count == col_count:
        sigma_jj = finish_diagonal(update, jj_inverse, col_count)
    else:
        update = jnp.where(col_index == root_col, update, 0.0)
        update = lax.psum_scatter(update, "col", scatter_dimension=2, tiled=True)
        sigma_jj = jj_inverse - lax.psum(update, "row")
    return (jnp.stack(rj_list), sigma_jj)


def solution(mesh):
    placed = (
        P(("parts", "row"), "col"),
        P("parts", ("col", "row"), None),
        P("parts", None, "col"),
        P("parts", None),
    )
    return jax.shard_map(
        shards,
        mesh=mesh,
        in_specs=placed,
        out_specs=(P("parts", "row", "col"), P("parts", None, "col")),
        check_vma=False,
    )
```

```python
import functools

import jax
import jax.numpy as jnp
from jax import lax
from jax.experimental import pallas as pl
from jax.experimental.pallas import tpu as pltpu
from jax.sharding import PartitionSpec as P

BLK = 48
HALVES = 2
MESH = pl.DeviceIdType.MESH


def listed_mask(blocks, first_block, count, rows):
    block_ids = first_block + jnp.arange(count, dtype=jnp.int32)
    listed = jnp.any(blocks[:, :, None] == block_ids[None, None, :], axis=1).astype(jnp.float32)
    return jnp.repeat(listed, BLK, axis=1, total_repeat_length=rows)


def split(value):
    high = lax.reduce_precision(value, 8, 7)
    return high.astype(jnp.bfloat16), (value - high).astype(jnp.bfloat16)


def dot3(left, right, dims):
    (lh, ll), (rh, rl) = left, right

    def dot(a, b):
        return lax.dot_general(a, b, (dims, ((), ())), preferred_element_type=jnp.float32)

    return dot(lh, rh) + dot(lh, rl) + dot(ll, rh)


def diagonal_kernel(n, u_ref, jj_ref, out_ref, held, send1, recv1, send2, recv2):
    row, col = lax.axis_index("row"), lax.axis_index("col")
    me = row * n + col
    count = n * n
    piece = u_ref.shape[1] // n
    width = u_ref.shape[2] // n
    barrier = pltpu.get_barrier_semaphore()
    for step in range(1, count):
        other = lax.rem(me + step, count)
        pl.semaphore_signal(barrier, inc=1, device_id={"row": other // n, "col": lax.rem(other, n)}, device_id_type=MESH)
    pl.semaphore_wait(barrier, count - 1)

    def part_of(to_row, to_col):
        return u_ref.at[:, pl.ds(pl.multiple_of(to_row * piece, piece), piece), pl.ds(pl.multiple_of(to_col * width, width), width)]

    def scatter(step):
        other = lax.rem(me + step, count)
        to_row, to_col = other // n, lax.rem(other, n)
        return pltpu.make_async_remote_copy(
            src_ref=part_of(to_row, to_col),
            dst_ref=held.at[row],
            send_sem=send1.at[step],
            recv_sem=recv1.at[row],
            device_id={"row": to_row, "col": to_col},
            device_id_type=MESH,
        )

    @pl.when(row == col)
    def _():
        for step in range(1, count):
            scatter(step).start()
        held[row] = part_of(row, col)[...]

    for root in range(n):
        @pl.when(jnp.logical_or(row != root, col != root))
        def _():
            pltpu.make_async_remote_copy(
                src_ref=held.at[root],
                dst_ref=held.at[root],
                send_sem=send1.at[0],
                recv_sem=recv1.at[root],
                device_id={"row": lax.rem(row + 1, n)},
                device_id_type=MESH,
            ).wait_recv()

    mine = pl.ds(pl.multiple_of(row * piece, piece), piece)
    total = held[0]
    for root in range(1, n):
        total = total + held[root]
    out_ref[:, mine, :] = jj_ref[:, mine, :] - total

    def share(step):
        return pltpu.make_async_remote_copy(
            src_ref=out_ref.at[:, mine, :],
            dst_ref=out_ref.at[:, mine, :],
            send_sem=send2.at[step],
            recv_sem=recv2.at[step],
            device_id={"row": lax.rem(row + step, n)},
            device_id_type=MESH,
        )

    for step in range(1, n):
        share(step).start()
    for step in range(1, n):
        share(step).wait()

    @pl.when(row == col)
    def _():
        for step in range(1, count):
            scatter(step).wait_send()


def finish_diagonal(update, jj_inverse, n):
    supernodes, w, part_cols = jj_inverse.shape
    return pl.pallas_call(
        functools.partial(diagonal_kernel, n),
        out_shape=jax.ShapeDtypeStruct(jj_inverse.shape, jnp.float32),
        in_specs=[pl.BlockSpec(memory_space=pltpu.VMEM)] * 2,
        out_specs=pl.BlockSpec(memory_space=pltpu.VMEM),
        scratch_shapes=[
            pltpu.VMEM((n, supernodes, w // n, part_cols), jnp.float32),
            pltpu.SemaphoreType.DMA((n * n,)),
            pltpu.SemaphoreType.DMA((n,)),
            pltpu.SemaphoreType.DMA((n,)),
            pltpu.SemaphoreType.DMA((n,)),
        ],
        compiler_params=pltpu.CompilerParams(collective_id=0, has_side_effects=True),
    )(update, jj_inverse)


def product_kernel(a_ref, b_ref, scale_ref, out_ref, bh_ref, bl_ref):
    @pl.when(pl.program_id(0) == 0)
    def _():
        b = b_ref[...]
        high = b.astype(jnp.bfloat16)
        bh_ref[...] = high
        bl_ref[...] = (b - high.astype(jnp.float32)).astype(jnp.bfloat16)

    a = a_ref[...]
    ah = a.astype(jnp.bfloat16)
    al = (a - ah.astype(jnp.float32)).astype(jnp.bfloat16)
    total = jnp.dot(ah, bh_ref[...], preferred_element_type=jnp.float32)
    total += jnp.dot(ah, bl_ref[...], preferred_element_type=jnp.float32)
    total += jnp.dot(al, bh_ref[...], preferred_element_type=jnp.float32)
    out_ref[...] = total.T * scale_ref[...]


def product(a, b, scale):
    rows, depth = a.shape
    columns = b.shape[1]
    tile = 256 if rows % 256 == 0 else rows
    return pl.pallas_call(
        product_kernel,
        grid=(rows // tile,),
        out_shape=jax.ShapeDtypeStruct((columns, rows), jnp.float32),
        in_specs=[
            pl.BlockSpec((tile, depth), lambda i: (i, 0)),
            pl.BlockSpec((depth, columns), lambda i: (0, 0)),
            pl.BlockSpec((1, tile), lambda i: (0, i)),
        ],
        out_specs=pl.BlockSpec((columns, tile), lambda i: (0, i)),
        scratch_shapes=[pltpu.VMEM((depth, columns), jnp.bfloat16)] * 2,
        compiler_params=pltpu.CompilerParams(vmem_limit_bytes=40 * 1024 * 1024),
        cost_estimate=pl.CostEstimate(
            flops=6 * rows * depth * columns, bytes_accessed=4 * rows * depth, transcendentals=0
        ),
    )(a, b, scale)


def swap(value, distance):
    return lax.ppermute(value, "col", [(i, i ^ distance) for i in range(lax.axis_size("col"))])


def scatter_sum(partial, col_index):
    if lax.axis_size("col") != 4:
        return lax.psum_scatter(partial, "col", scatter_dimension=0, tiled=True)
    pieces = partial.reshape(2, 2, partial.shape[0] // 4, partial.shape[1])
    far, near = col_index // 2, col_index % 2
    sent = lax.dynamic_index_in_dim(pieces, 1 - near, 1, keepdims=False)
    summed = lax.dynamic_index_in_dim(pieces, near, 1, keepdims=False) + swap(sent, 1)
    sent = lax.dynamic_index_in_dim(summed, 1 - far, 0, keepdims=False)
    return lax.dynamic_index_in_dim(summed, far, 0, keepdims=False) + swap(sent, 2)


def widen(own, col_index):
    if lax.axis_size("col") != 4:
        return lax.all_gather(own, "col", axis=0, tiled=True)
    far, near = col_index // 2, col_index % 2
    other = swap(own, 2)
    pair = jnp.stack([jnp.where(far == 0, own, other), jnp.where(far == 0, other, own)])
    across = swap(pair, 1)
    wide = jnp.stack([jnp.where(near == 0, pair, across), jnp.where(near == 0, across, pair)], axis=1)
    return wide.reshape(4 * own.shape[0], own.shape[1])


def shards(sigma_anc, normal_factor, jj_inverse, blocks):
    tile_rows, tile_cols = sigma_anc.shape
    row_count = lax.axis_size("row")
    col_count = lax.axis_size("col")
    row_index = lax.axis_index("row")
    col_index = lax.axis_index("col")
    supernodes, local_rows, w = normal_factor.shape
    part_cols = jj_inverse.shape[2]
    sub = part_cols // HALVES
    chunk = sub * col_count
    local_blocks = local_rows // BLK
    first_local = (col_index * row_count + row_index) * local_blocks
    masked = normal_factor * listed_mask(blocks, first_local, local_blocks, local_rows)[:, :, None]
    chunks = masked.reshape(supernodes, local_rows, col_count, HALVES, sub).transpose(0, 3, 1, 2, 4)
    chunks = chunks.reshape(supernodes, HALVES, local_rows, chunk)
    row_blocks = tile_rows // BLK
    row_mask = listed_mask(blocks, row_index * row_blocks, row_blocks, tile_rows)
    start_row = row_index * tile_rows
    root_col = start_row // tile_cols
    square = tile_rows == tile_cols
    offset = jnp.clip(start_row - col_index * tile_cols, 0, tile_cols - tile_rows)

    def slab_of(value):
        return value if square else lax.dynamic_slice_in_dim(value, offset, tile_rows, 0)

    order = [(supernode, half) for supernode in range(supernodes) for half in range(HALVES)]
    own_list = []
    wide_list = []
    slab_list = []
    for at, (supernode, half) in enumerate(order):
        local = chunks[supernode, half]
        if at >= 2:
            local, own_list[at - 2] = lax.optimization_barrier((local, own_list[at - 2]))
        gathered = lax.all_gather(local, "row", axis=0, tiled=True)
        if at >= 2:
            gathered, own_list[at - 1], wide_list[at - 2] = lax.optimization_barrier(
                (gathered, own_list[at - 1], wide_list[at - 2])
            )
        elif at >= 1:
            gathered, own_list[at - 1] = lax.optimization_barrier((gathered, own_list[at - 1]))
        own_list.append(scatter_sum(product(sigma_anc, gathered, -row_mask[supernode][None, :]), col_index))
        wide_list.append(widen(own_list[at], col_index))
        slab_list.append(split(slab_of(gathered)))
    rj_list = []
    update_list = []
    for supernode in range(supernodes):
        own = own_list[HALVES * supernode:HALVES * (supernode + 1)]
        rj_list.append(jnp.concatenate(own, axis=0).T)
        pieces = slab_list[HALVES * supernode:HALVES * (supernode + 1)]
        slab = tuple(jnp.concatenate([piece[i] for piece in pieces], axis=1) for i in range(2))
        wides = wide_list[HALVES * supernode:HALVES * (supernode + 1)]
        update = jnp.stack([dot3(slab, split(wide), ((0,), (1,))) for wide in wides], axis=1)
        update = update.reshape(HALVES, col_count, sub, HALVES, col_count, sub).transpose(1, 0, 2, 4, 3, 5)
        update_list.append(update.reshape(w, w))
    update = jnp.stack(update_list)
    if square and row_count == col_count:
        sigma_jj = finish_diagonal(update, jj_inverse, col_count)
    else:
        update = jnp.where(col_index == root_col, update, 0.0)
        update = lax.psum_scatter(update, "col", scatter_dimension=2, tiled=True)
        sigma_jj = jj_inverse - lax.psum(update, "row")
    return (jnp.stack(rj_list), sigma_jj)


def solution(mesh):
    placed = (
        P(("parts", "row"), "col"),
        P("parts", ("col", "row"), None),
        P("parts", None, "col"),
        P("parts", None),
    )
    return jax.shard_map(
        shards,
        mesh=mesh,
        in_specs=placed,
        out_specs=(P("parts", "row", "col"), P("parts", None, "col")),
        check_vma=False,
    )
```

```python
import functools

import jax
import jax.numpy as jnp
from jax import lax
from jax.experimental import pallas as pl
from jax.experimental.pallas import tpu as pltpu
from jax.sharding import PartitionSpec as P

BLK = 48
HALVES = 2
MESH = pl.DeviceIdType.MESH


def listed_mask(blocks, first_block, count, rows):
    block_ids = first_block + jnp.arange(count, dtype=jnp.int32)
    listed = jnp.any(blocks[:, :, None] == block_ids[None, None, :], axis=1).astype(jnp.float32)
    return jnp.repeat(listed, BLK, axis=1, total_repeat_length=rows)


def split(value):
    high = lax.reduce_precision(value, 8, 7)
    return high.astype(jnp.bfloat16), (value - high).astype(jnp.bfloat16)


def dot3(left, right, dims):
    (lh, ll), (rh, rl) = left, right

    def dot(a, b):
        return lax.dot_general(a, b, (dims, ((), ())), preferred_element_type=jnp.float32)

    return dot(lh, rh) + dot(lh, rl) + dot(ll, rh)


def diagonal_kernel(n, u_ref, jj_ref, out_ref, held, send1, recv1, send2, recv2):
    row, col = lax.axis_index("row"), lax.axis_index("col")
    me = row * n + col
    count = n * n
    piece = u_ref.shape[1] // n
    width = u_ref.shape[2] // n
    barrier = pltpu.get_barrier_semaphore()
    for step in range(1, count):
        other = lax.rem(me + step, count)
        pl.semaphore_signal(barrier, inc=1, device_id={"row": other // n, "col": lax.rem(other, n)}, device_id_type=MESH)
    pl.semaphore_wait(barrier, count - 1)

    def part_of(to_row, to_col):
        return u_ref.at[:, pl.ds(pl.multiple_of(to_row * piece, piece), piece), pl.ds(pl.multiple_of(to_col * width, width), width)]

    def scatter(step):
        other = lax.rem(me + step, count)
        to_row, to_col = other // n, lax.rem(other, n)
        return pltpu.make_async_remote_copy(
            src_ref=part_of(to_row, to_col),
            dst_ref=held.at[row],
            send_sem=send1.at[step],
            recv_sem=recv1.at[row],
            device_id={"row": to_row, "col": to_col},
            device_id_type=MESH,
        )

    @pl.when(row == col)
    def _():
        for step in range(1, count):
            scatter(step).start()
        held[row] = part_of(row, col)[...]

    for root in range(n):
        @pl.when(jnp.logical_or(row != root, col != root))
        def _():
            pltpu.make_async_remote_copy(
                src_ref=held.at[root],
                dst_ref=held.at[root],
                send_sem=send1.at[0],
                recv_sem=recv1.at[root],
                device_id={"row": lax.rem(row + 1, n)},
                device_id_type=MESH,
            ).wait_recv()

    mine = pl.ds(pl.multiple_of(row * piece, piece), piece)
    total = held[0]
    for root in range(1, n):
        total = total + held[root]
    out_ref[:, mine, :] = jj_ref[:, mine, :] - total

    def share(step):
        return pltpu.make_async_remote_copy(
            src_ref=out_ref.at[:, mine, :],
            dst_ref=out_ref.at[:, mine, :],
            send_sem=send2.at[step],
            recv_sem=recv2.at[step],
            device_id={"row": lax.rem(row + step, n)},
            device_id_type=MESH,
        )

    for step in range(1, n):
        share(step).start()
    for step in range(1, n):
        share(step).wait()

    @pl.when(row == col)
    def _():
        for step in range(1, count):
            scatter(step).wait_send()


def finish_diagonal(update, jj_inverse, n):
    supernodes, w, part_cols = jj_inverse.shape
    return pl.pallas_call(
        functools.partial(diagonal_kernel, n),
        out_shape=jax.ShapeDtypeStruct(jj_inverse.shape, jnp.float32),
        in_specs=[pl.BlockSpec(memory_space=pltpu.VMEM)] * 2,
        out_specs=pl.BlockSpec(memory_space=pltpu.VMEM),
        scratch_shapes=[
            pltpu.VMEM((n, supernodes, w // n, part_cols), jnp.float32),
            pltpu.SemaphoreType.DMA((n * n,)),
            pltpu.SemaphoreType.DMA((n,)),
            pltpu.SemaphoreType.DMA((n,)),
            pltpu.SemaphoreType.DMA((n,)),
        ],
        compiler_params=pltpu.CompilerParams(collective_id=0, has_side_effects=True),
    )(update, jj_inverse)


def product_kernel(a_ref, b_ref, scale_ref, out_ref, bh_ref, bl_ref):
    @pl.when(pl.program_id(0) == 0)
    def _():
        b = b_ref[...]
        high = b.astype(jnp.bfloat16)
        bh_ref[...] = high
        bl_ref[...] = (b - high.astype(jnp.float32)).astype(jnp.bfloat16)

    a = a_ref[...]
    ah = a.astype(jnp.bfloat16)
    al = (a - ah.astype(jnp.float32)).astype(jnp.bfloat16)
    total = jnp.dot(ah, bh_ref[...], preferred_element_type=jnp.float32)
    total += jnp.dot(ah, bl_ref[...], preferred_element_type=jnp.float32)
    total += jnp.dot(al, bh_ref[...], preferred_element_type=jnp.float32)
    out_ref[...] = total.T * scale_ref[...]


def product(a, b, scale):
    rows, depth = a.shape
    columns = b.shape[1]
    tile = 256 if rows % 256 == 0 else rows
    return pl.pallas_call(
        product_kernel,
        grid=(rows // tile,),
        out_shape=jax.ShapeDtypeStruct((columns, rows), jnp.float32),
        in_specs=[
            pl.BlockSpec((tile, depth), lambda i: (i, 0)),
            pl.BlockSpec((depth, columns), lambda i: (0, 0)),
            pl.BlockSpec((1, tile), lambda i: (0, i)),
        ],
        out_specs=pl.BlockSpec((columns, tile), lambda i: (0, i)),
        scratch_shapes=[pltpu.VMEM((depth, columns), jnp.bfloat16)] * 2,
        compiler_params=pltpu.CompilerParams(vmem_limit_bytes=40 * 1024 * 1024),
        cost_estimate=pl.CostEstimate(
            flops=6 * rows * depth * columns, bytes_accessed=4 * rows * depth, transcendentals=0
        ),
    )(a, b, scale)


def swap(value, distance):
    return lax.ppermute(value, "col", [(i, i ^ distance) for i in range(lax.axis_size("col"))])


def scatter_sum(partial, col_index):
    if lax.axis_size("col") != 4:
        return lax.psum_scatter(partial, "col", scatter_dimension=0, tiled=True)
    pieces = partial.reshape(2, 2, partial.shape[0] // 4, partial.shape[1])
    far, near = col_index // 2, col_index % 2
    sent = lax.dynamic_index_in_dim(pieces, 1 - near, 1, keepdims=False)
    summed = lax.dynamic_index_in_dim(pieces, near, 1, keepdims=False) + swap(sent, 1)
    sent = lax.dynamic_index_in_dim(summed, 1 - far, 0, keepdims=False)
    return lax.dynamic_index_in_dim(summed, far, 0, keepdims=False) + swap(sent, 2)


def widen(own, col_index):
    if lax.axis_size("col") != 4:
        return lax.all_gather(own, "col", axis=0, tiled=True)
    far, near = col_index // 2, col_index % 2
    other = swap(own, 2)
    pair = jnp.stack([jnp.where(far == 0, own, other), jnp.where(far == 0, other, own)])
    across = swap(pair, 1)
    wide = jnp.stack([jnp.where(near == 0, pair, across), jnp.where(near == 0, across, pair)], axis=1)
    return wide.reshape(4 * own.shape[0], own.shape[1])


def shards(sigma_anc, normal_factor, jj_inverse, blocks):
    tile_rows, tile_cols = sigma_anc.shape
    row_count = lax.axis_size("row")
    col_count = lax.axis_size("col")
    row_index = lax.axis_index("row")
    col_index = lax.axis_index("col")
    supernodes, local_rows, w = normal_factor.shape
    part_cols = jj_inverse.shape[2]
    sub = part_cols // HALVES
    chunk = sub * col_count
    local_blocks = local_rows // BLK
    first_local = (col_index * row_count + row_index) * local_blocks
    masked = normal_factor * listed_mask(blocks, first_local, local_blocks, local_rows)[:, :, None]
    chunks = masked.reshape(supernodes, local_rows, col_count, HALVES, sub).transpose(0, 3, 1, 2, 4)
    chunks = chunks.reshape(supernodes, HALVES, local_rows, chunk)
    row_blocks = tile_rows // BLK
    row_mask = listed_mask(blocks, row_index * row_blocks, row_blocks, tile_rows)
    start_row = row_index * tile_rows
    root_col = start_row // tile_cols
    square = tile_rows == tile_cols
    offset = jnp.clip(start_row - col_index * tile_cols, 0, tile_cols - tile_rows)

    def slab_of(value):
        return value if square else lax.dynamic_slice_in_dim(value, offset, tile_rows, 0)

    order = [(supernode, half) for supernode in range(supernodes) for half in range(HALVES)]
    own_list = []
    wide_list = []
    slab_list = []
    for at, (supernode, half) in enumerate(order):
        local = chunks[supernode, half]
        gathered = lax.all_gather(local, "row", axis=0, tiled=True)
        if at >= 2:
            gathered, own_list[at - 1], wide_list[at - 2] = lax.optimization_barrier(
                (gathered, own_list[at - 1], wide_list[at - 2])
            )
        elif at >= 1:
            gathered, own_list[at - 1] = lax.optimization_barrier((gathered, own_list[at - 1]))
        own_list.append(scatter_sum(product(sigma_anc, gathered, -row_mask[supernode][None, :]), col_index))
        wide_list.append(widen(own_list[at], col_index))
        slab_list.append(split(slab_of(gathered)))
    rj_list = []
    update_list = []
    for supernode in range(supernodes):
        own = own_list[HALVES * supernode:HALVES * (supernode + 1)]
        rj_list.append(jnp.concatenate(own, axis=0).T)
        pieces = slab_list[HALVES * supernode:HALVES * (supernode + 1)]
        slab = tuple(jnp.concatenate([piece[i] for piece in pieces], axis=1) for i in range(2))
        wides = wide_list[HALVES * supernode:HALVES * (supernode + 1)]
        update = jnp.stack([dot3(slab, split(wide), ((0,), (1,))) for wide in wides], axis=1)
        update = update.reshape(HALVES, col_count, sub, HALVES, col_count, sub).transpose(1, 0, 2, 4, 3, 5)
        update_list.append(update.reshape(w, w))
    update = jnp.stack(update_list)
    if square and row_count == col_count:
        sigma_jj = finish_diagonal(update, jj_inverse, col_count)
    else:
        update = jnp.where(col_index == root_col, update, 0.0)
        update = lax.psum_scatter(update, "col", scatter_dimension=2, tiled=True)
        sigma_jj = jj_inverse - lax.psum(update, "row")
    return (jnp.stack(rj_list), sigma_jj)


def solution(mesh):
    placed = (
        P(("parts", "row"), "col"),
        P("parts", ("col", "row"), None),
        P("parts", None, "col"),
        P("parts", None),
    )
    return jax.shard_map(
        shards,
        mesh=mesh,
        in_specs=placed,
        out_specs=(P("parts", "row", "col"), P("parts", None, "col")),
        check_vma=False,
    )
```
